32 devices in a mesh: grp: 2 (over x), dev: 16 (over z, y, core).
Axes of the slice: x: 2, y: 2, z: 4, core: 2. Of those that a mesh axis runs over, the one named last changes fastest.
Arguments:
- query: bfloat16 [64, 64, 128], P(('grp', 'dev')), may hold values from -6 to 6
- key_cache: bfloat16 [64, 512, 8, 128], P(('grp', 'dev')), may hold values from -6 to 6
- value_cache: bfloat16 [64, 512, 8, 128], P(('grp', 'dev')), may hold values from -6 to 6
- lengths: int32 [64], P(('grp', 'dev')), may hold values from 1 to 512, 16384 in all
- out_weight: bfloat16 [8192, 8192], P('dev', 'grp'), may hold values from -0.0625 to 0.0625
- resid: bfloat16 [64, 8192], P('dev', 'grp'), may hold values from -6 to 6
- norm_gain: bfloat16 [8192], P('grp'), may hold values from 0.5 to 1.5
- gate_weight: bfloat16 [8192, 28672], P('grp', 'dev'), may hold values from -0.0625 to 0.0625
- up_weight: bfloat16 [8192, 28672], P('grp', 'dev'), may hold values from -0.0625 to 0.0625
- down_weight: bfloat16 [28672, 8192], P('dev', 'grp'), may hold values from -0.03125 to 0.03125
Outputs:
- layer_out: bfloat16 [64, 8192], P('dev', 'grp')
The draws below stay inside these ranges and needn't reach their ends.
Inputs may be any that keep to these rules, and one draw needn't show every extreme that they name: `lengths`: some request has exactly 512 live slots.
All inputs are finite; a program needn't handle non-finite values. No bound on the sum of `lengths` on one device may be relied on, other than what follows from the above.
Results may differ from the reference program's by a relative error of at most 0.015.
Values may be sent and summed in bfloat16 or wider, within the bound.
A program may use at most 128 MiB of HBM per device.

```python
import math
import jax
import jax.numpy as jnp
import numpy as np
from jax import lax

D = 8192
FF = 28672
QH = 64
KVH = 8
HD = 128
CTX = 512
TOKENS = 64


def draw_query(key, part):
    base = jnp.clip(jax.random.normal(jax.random.fold_in(key, 3), (TOKENS, QH, HD), jnp.float32), -5.5, 5.5)
    return base.astype(jnp.bfloat16)


def draw_key_cache(key, part):
    base = jnp.clip(jax.random.normal(jax.random.fold_in(key, 5), (TOKENS, CTX, KVH, HD), jnp.float32), -5.5, 5.5)
    return base.astype(jnp.bfloat16)


def level_of(rng, dims, split, smallest, high):
    def one(position, shards_of):
        steps = jax.random.uniform(jax.random.fold_in(jax.random.fold_in(rng, 6), position), (shards_of,), jnp.float32, smallest / len(split), high / len(split))
        return jnp.repeat(jnp.exp(steps), dims[position] // shards_of).reshape((-1,) + (1,) * (len(dims) - position - 1))

    level = one(*split[0])
    for cut in split[1:]:
        level = level * one(*cut)
    return level


def profile(number_of, total, bound, slope):
    portions = [(1 << 20) // math.isqrt(rank ** slope) + 1 for rank in range(2, number_of + 1)]
    spare, given = total - bound - (number_of - 1), [1] * (number_of - 1)
    while spare > 0:
        candidates = [i for i in range(number_of - 1) if given[i] < bound]
        whole, budget = sum([portions[i] for i in candidates]), spare
        for i in candidates:
            more = min(bound - given[i], max(1, budget * portions[i] // whole), spare)
            given[i] = given[i] + more
            spare = spare - more
    return np.array([bound] + given)


def uneven(rng, count, total, most, slope):
    if count == 2:
        one = jax.random.randint(rng, (), max(1, total - most), min(most, total - 1) + 1)
        return jnp.stack([one, total - one])
    tallies = jnp.asarray(profile(count, total, most, slope), jnp.int32)
    pairs = (count - 1) // 2
    giver, taker = tallies[1:1 + 2 * pairs:2], tallies[2:2 + 2 * pairs:2]
    margin = jnp.minimum(giver - 1, most - taker)
    moved = jax.random.randint(jax.random.fold_in(rng, 1), (pairs,), 0, 1 << 20) % (margin + 1)
    tallies = tallies.at[1:1 + 2 * pairs:2].set(giver - moved).at[2:2 + 2 * pairs:2].set(taker + moved)
    return tallies[jax.random.permutation(jax.random.fold_in(rng, 2), count)]


def scatter_about(rng, extent, deviation, most, split=(), kind=jnp.bfloat16):
    entries = deviation * jax.random.normal(rng, extent, jnp.float32)
    if split:
        entries = entries * level_of(rng, extent, split, -0.22, 0.18)
    return jnp.clip(entries, -most, most).astype(kind)


def setup_inputs(seed: int = 0) -> dict:
    seeds = jax.random.split(jax.random.key(seed), 11)
    return {
        "query": draw_query(jax.random.fold_in(seeds[10], 71), 0),
        "key_cache": draw_key_cache(jax.random.fold_in(seeds[10], 71), 0),
        "value_cache": scatter_about(seeds[2], (TOKENS, CTX, KVH, HD), 1.0, 6.0, ((0, 32),)),
        "lengths": uneven(seeds[3], TOKENS, TOKENS * CTX // 2, CTX, 2).astype(jnp.int32),
        "out_weight": scatter_about(seeds[4], (QH * HD, D), (QH * HD) ** -0.5, 0.0625, ((0, 16), (1, 2))),
        "resid": scatter_about(seeds[5], (TOKENS, D), 1.0, 6.0, ((0, 16), (1, 2))),
        "norm_gain": jnp.clip(1.0 + 0.1 * jax.random.normal(seeds[6], (D,), jnp.float32), 0.5, 1.5).astype(jnp.bfloat16),
        "gate_weight": scatter_about(seeds[7], (D, FF), D ** -0.5, 0.0625, ((0, 2), (1, 16))),
        "up_weight": scatter_about(seeds[8], (D, FF), D ** -0.5, 0.0625, ((0, 2), (1, 16))),
        "down_weight": scatter_about(seeds[9], (FF, D), FF ** -0.5, 0.03125, ((0, 16), (1, 2))),
    }


def attend_one(packed):
    query_row, key_rows, value_rows, length = packed
    group = QH // KVH
    query_f = query_row.astype(jnp.float32).reshape(KVH, group, HD)
    keys_f = key_rows.astype(jnp.float32)
    scores = jnp.einsum('hgd,lhd->hgl', query_f, keys_f) * HD ** (-0.5)
    places = jnp.arange(CTX, dtype=jnp.int32)
    valid = places < length
    scores = jnp.where(valid[None, None, :], scores, -1e+30)
    top = lax.optimization_barrier(jnp.max(scores, axis=-1, keepdims=True))
    weights = jnp.exp(scores - top)
    probs = (weights / lax.optimization_barrier(jnp.sum(weights, axis=-1, keepdims=True))).astype(jnp.bfloat16)
    mixed = jnp.einsum('hgl,lhd->hgd', probs.astype(jnp.float32), value_rows.astype(jnp.float32))
    return mixed.reshape(QH * HD).astype(jnp.bfloat16)

def reference(query, key_cache, value_cache, lengths, out_weight, resid, norm_gain, gate_weight, up_weight, down_weight):
    attn = lax.map(attend_one, (query, key_cache, value_cache, lengths))
    x = resid.astype(jnp.float32) + jnp.dot(attn, out_weight, preferred_element_type=jnp.float32)
    meansq = lax.optimization_barrier(jnp.mean(x * x, axis=1))
    normed = (x * lax.rsqrt(meansq + 1e-05)[:, None] * norm_gain.astype(jnp.float32)).astype(jnp.bfloat16)
    gate = jnp.dot(normed, gate_weight, preferred_element_type=jnp.float32)
    up = jnp.dot(normed, up_weight, preferred_element_type=jnp.float32)
    hidden = (jax.nn.silu(gate) * up).astype(jnp.bfloat16)
    total = x + jnp.dot(hidden, down_weight, preferred_element_type=jnp.float32)
    return total.astype(jnp.bfloat16)
```

```python
import functools

import jax
import jax.numpy as jnp
from jax import lax
from jax.experimental import pallas as pl
from jax.experimental.pallas import tpu as pltpu
from jax.sharding import PartitionSpec as P

MESH = pl.DeviceIdType.MESH
F32 = jnp.float32
BF16 = jnp.bfloat16


def attend(query, key_cache, value_cache, lengths):
    rows, heads, width = query.shape
    kv_heads = key_cache.shape[2]
    group = heads // kv_heads
    grouped = query.reshape(rows, kv_heads, group, width)
    scores = jnp.einsum(
        "rhgd,rlhd->rhgl", grouped, key_cache, preferred_element_type=jnp.float32
    ) * width ** (-0.5)
    places = jnp.arange(key_cache.shape[1], dtype=jnp.int32)
    valid = places[None, :] < lengths[:, None]
    scores = jnp.where(valid[:, None, None, :], scores, -1e30)
    top = jnp.max(scores, axis=-1, keepdims=True)
    weights = jnp.exp(scores - top)
    probs = (weights / jnp.sum(weights, axis=-1, keepdims=True)).astype(jnp.bfloat16)
    mixed = jnp.einsum("rhgl,rlhd->rhgd", probs, value_cache, preferred_element_type=jnp.float32)
    return mixed.reshape(rows, heads * width).astype(jnp.bfloat16)


def per_device(
    query,
    key_cache,
    value_cache,
    lengths,
    out_weight,
    resid,
    norm_gain,
    gate_weight,
    up_weight,
    down_weight,
):
    attn = attend(query, key_cache, value_cache, lengths)
    block_cols = out_weight.shape[0]
    first_col = lax.axis_index("dev") * block_cols
    cols = lax.dynamic_slice_in_dim(
        lax.all_gather(attn, ("grp", "dev"), axis=0, tiled=True), first_col, block_cols, 1
    )
    proj_terms = jnp.dot(cols, out_weight, preferred_element_type=jnp.float32)
    x = resid.astype(jnp.float32) + lax.psum_scatter(
        proj_terms, "dev", scatter_dimension=0, tiled=True
    )
    width_all = x.shape[1] * lax.axis_size("grp")
    sumsq = lax.psum(jnp.sum(x * x, axis=1), "grp")
    normed = (
        x * lax.rsqrt(sumsq / width_all + 1e-05)[:, None] * norm_gain.astype(jnp.float32)
    ).astype(jnp.bfloat16)
    piece = lax.all_gather(normed, "dev", axis=0, tiled=True)
    half_terms = jnp.concatenate(
        [
            jnp.dot(piece, gate_weight, preferred_element_type=jnp.float32),
            jnp.dot(piece, up_weight, preferred_element_type=jnp.float32),
        ],
        axis=1,
    )
    both = lax.psum(half_terms.astype(jnp.bfloat16), "grp").astype(jnp.float32)
    hidden_cols = gate_weight.shape[1]
    gate = both[:, :hidden_cols]
    up = both[:, hidden_cols:]
    hidden = (jax.nn.silu(gate) * up).astype(jnp.bfloat16)
    ffn_rows = lax.psum_scatter(
        jnp.dot(hidden, down_weight, preferred_element_type=jnp.float32),
        "dev",
        scatter_dimension=0,
        tiled=True,
    )
    return (x + ffn_rows).astype(jnp.bfloat16)


def remote(src, dst, send, recv, **where):
    return pltpu.make_async_remote_copy(
        src_ref=src, dst_ref=dst, send_sem=send, recv_sem=recv,
        device_id=where, device_id_type=MESH,
    )


def loop(n, f):
    def step(i, carry):
        f(i)
        return carry

    lax.fori_loop(0, n, step, 0)


def layer_kernel(
    nd,
    len_ref, q_ref, k_hbm, v_hbm, wo_hbm, resid_ref, gain_ref, wg_hbm, wu_hbm, wd_hbm,
    out_ref,
    kb, vb, wo, wg, wu, wd,
    sc, ast, abuf, arecv, af, lhs, rbuf,
    psend, prec, pown, csend, crecv, xf, xall, xg, ssq,
    gsend, grecv, hid, hcat,
    psend2, prec2, csend2, crecv2, fin,
    kvsem, wsem, xs, rs, as_, ar, p1s, p1r, c1s, c1r, ags, agr, fws, fwr,
    gs, gr, hs, hr, p2s, p2r, c2s, c2r, fs,
):
    nc = nd // 2
    g = lax.axis_index("grp")
    d = lax.axis_index("dev")
    c = d // 2
    k = lax.rem(d, 2)
    og = 1 - g
    ok = 1 - k
    pair = c * 2 + ok
    rows = nd * 4
    half = wo.shape[1] // 2
    nn = half // 512
    units = wg.shape[1] // 2
    nu = units // 128
    heads = q_ref.shape[1]
    slots = k_hbm.shape[1]
    width_all = wo.shape[1] * 2

    barrier = pltpu.get_barrier_semaphore()
    pl.semaphore_signal(barrier, inc=1, device_id={"grp": og}, device_id_type=MESH)

    def greet(i):
        pl.semaphore_signal(
            barrier, inc=1, device_id={"dev": lax.rem(d + i + 1, nd)}, device_id_type=MESH
        )

    loop(nd - 1, greet)

    kv = []
    for r in range(2):
        kv.append((
            pltpu.make_async_copy(k_hbm.at[r], kb.at[r], kvsem.at[2 * r]),
            pltpu.make_async_copy(v_hbm.at[r], vb.at[r], kvsem.at[2 * r + 1]),
        ))
    for a, b in kv:
        a.start()
        b.start()
    wo_copy = pltpu.make_async_copy(wo_hbm, wo, wsem.at[0])
    wo_copy.start()
    ucols = [pl.ds(pl.multiple_of(og * units, 128), units), pl.ds(pl.multiple_of(g * units, 128), units)]
    gu_copies = []
    for i in range(2):
        gu_copies.append((
            pltpu.make_async_copy(wg_hbm.at[:, ucols[i]], wg.at[:, ucols[i]], wsem.at[1 + 2 * i]),
            pltpu.make_async_copy(wu_hbm.at[:, ucols[i]], wu.at[:, ucols[i]], wsem.at[2 + 2 * i]),
        ))
    wd_copy = pltpu.make_async_copy(wd_hbm, wd, wsem.at[5])

    piece = 1024
    np_ = slots // piece
    for r in range(2):
        kv[r][0].wait()
        q = q_ref[r]
        length = len_ref[r]
        row_head = lax.broadcasted_iota(jnp.int32, (heads, piece), 0) // 8
        col = lax.broadcasted_iota(jnp.int32, (heads, piece), 1)
        own = lax.rem(col, 8) == row_head
        place = col // 8
        top = jnp.full((heads, 1), -1e30, F32)
        for n in range(np_):
            s = lax.dot_general(
                q, kb[r, n * piece:(n + 1) * piece, :], (((1,), (1,)), ((), ())),
                preferred_element_type=F32,
            ) * (128 ** -0.5)
            live = own & (place + n * (piece // 8) < length)
            s = jnp.where(live, s, -1e30)
            sc[:, n * piece:(n + 1) * piece] = s
            top = jnp.maximum(top, jnp.max(s, axis=1, keepdims=True))
        kv[r][1].wait()
        if r == 1:
            for a, b in gu_copies:
                a.start()
                b.start()
            wd_copy.start()
        total = jnp.zeros((heads, 1), F32)
        o = jnp.zeros((heads, 128), F32)
        for n in range(np_):
            w = jnp.exp(sc[:, n * piece:(n + 1) * piece] - top)
            total = total + jnp.sum(w, axis=1, keepdims=True)
            o = o + jnp.dot(w.astype(BF16), vb[r, n * piece:(n + 1) * piece, :], preferred_element_type=F32)
        o = o / total
        for t in range(nd):
            ast[t, 4 * r:4 * r + 4, :] = o[4 * t:4 * t + 4, :]
    abuf[g] = ast[...].astype(BF16)

    pl.semaphore_wait(barrier, nd)
    xcopy = remote(abuf.at[g], abuf.at[g], xs.at[0], xs.at[1], grp=og)
    xcopy.start()
    rcopy = remote(resid_ref, rbuf.at[k], rs.at[0], rs.at[1], dev=pair)
    rcopy.start()
    rbuf[k] = resid_ref[...]
    xcopy.wait()

    def send_attn(i):
        to = lax.rem(d + i + 1, nd)
        remote(abuf.at[:, to], arecv.at[d], as_.at[to], ar.at[d], dev=to).start()

    loop(nd - 1, send_attn)
    arecv[d] = abuf[:, d]

    def take_attn(i):
        frm = lax.rem(d + i + 1, nd)
        remote(abuf.at[:, frm], arecv.at[frm], as_.at[frm], ar.at[frm], dev=frm).wait_recv()

    loop(nd - 1, take_attn)
    wo_copy.wait()
    for h in range(2):
        af[h * nd * 8:(h + 1) * nd * 8, :] = arecv[:, h].astype(F32).reshape(nd * 8, 128)
    for j in range(4):
        lhs[:, j * 128:(j + 1) * 128] = af[pl.ds(j, rows, stride=4), :].astype(BF16)

    def reduce_rows(left, w, ps, pr, cs, cr, pss, prs, css, crs, finish):
        def other(n):
            cols = pl.ds(pl.multiple_of(ok * half + n * 512, 512), 512)
            v = jnp.dot(left[...], w[:, cols], preferred_element_type=F32)
            ps[n] = v.reshape(nc, 8, 512).astype(BF16)
            remote(ps.at[n], pr.at[n], pss.at[n], prs.at[n], dev=pair).start()

        loop(nn, other)

        def mine(n):
            cols = pl.ds(pl.multiple_of(k * half + n * 512, 512), 512)
            v = jnp.dot(left[...], w[:, cols], preferred_element_type=F32)
            remote(ps.at[n], pr.at[n], pss.at[n], prs.at[n], dev=pair).wait_recv()
            v = v.reshape(nc, 8, 512) + pr[n].astype(F32)
            pown[n] = v
            cs[:, n] = v.astype(BF16)

        loop(nn, mine)

        def send(i):
            to = lax.rem(c + i + 1, nc)
            remote(cs.at[to], cr.at[c], css.at[to], crs.at[c], dev=to * 2 + k).start()

        loop(nc - 1, send)

        def take(i):
            frm = lax.rem(c + i + 1, nc)
            remote(cs.at[frm], cr.at[frm], css.at[frm], crs.at[frm], dev=frm * 2 + k).wait_recv()

        loop(nc - 1, take)
        for n in range(nn):
            v = pown[n, c]
            for i in range(1, nc):
                v = v + cr[lax.rem(c + i, nc), n].astype(F32)
            finish(n, v)

        def done_pair(n):
            remote(ps.at[n], pr.at[n], pss.at[n], prs.at[n], dev=pair).wait_send()

        def done(i):
            to = lax.rem(c + i + 1, nc)
            remote(cs.at[to], cr.at[c], css.at[to], crs.at[c], dev=to * 2 + k).wait_send()

        def drain():
            loop(nn, done_pair)
            loop(nc - 1, done)

        return drain

    rcopy.wait()

    def finish_x(n, v):
        cols = pl.ds(pl.multiple_of(k * half + n * 512, 512), 512)
        for h in range(2):
            xf[n, 4 * h:4 * h + 4, :] = rbuf[h, :, cols].astype(F32)
        v = v + xf[n]
        xf[n] = v
        xall[k, c, n] = (v * gain_ref[:, cols]).astype(BF16)

    drain1 = reduce_rows(lhs, wo, psend, prec, csend, crecv, p1s, p1r, c1s, c1r, finish_x)

    def ag_send(i):
        to = lax.rem(c + i + 1, nc)
        remote(xall.at[k, c], xall.at[k, c], ags.at[to], agr.at[c], dev=to * 2 + k).start()

    loop(nc - 1, ag_send)

    def forward(frm):
        return remote(xall.at[k, frm], xall.at[k, frm], fws.at[frm], fwr.at[frm], dev=pair)

    forward(c).start()

    def ag_take(i):
        frm = lax.rem(c + i + 1, nc)
        remote(xall.at[k, frm], xall.at[k, frm], ags.at[frm], agr.at[frm], dev=frm * 2 + k).wait_recv()
        forward(frm).start()

    loop(nc - 1, ag_take)
    drain1()

    def fw_take(i):
        remote(xall.at[ok, i], xall.at[ok, i], fws.at[i], fwr.at[i], dev=pair).wait_recv()

    loop(nc, fw_take)

    squares = jnp.zeros((rows, 128), F32)
    for h in range(2):
        for n in range(nn):
            v = xall[h, :, n].astype(F32).reshape(rows, 512)
            lo = h * half + n * 512
            xg[:, lo:lo + 512] = v.astype(BF16)
            v = v / gain_ref[:, lo:lo + 512]
            v = v * v
            for t in range(4):
                squares = squares + v[:, t * 128:(t + 1) * 128]
    ssq[g] = squares
    scopy = remote(ssq.at[g], ssq.at[g], xs.at[2], xs.at[3], grp=og)
    scopy.start()

    def gate_up(base, n):
        cols = pl.ds(pl.multiple_of(base + n * 128, 128), 128)
        both = jnp.concatenate([wg[:, cols], wu[:, cols]], axis=1)
        return jnp.dot(xg[...], both, preferred_element_type=F32)

    def gcopy(n):
        return remote(gsend.at[n], grecv.at[n], gs.at[n], gr.at[n], grp=og)

    def hcopy(n):
        return remote(hid.at[g, n], hid.at[g, n], hs.at[n], hr.at[n], grp=og)

    for cp in gu_copies[0]:
        cp.wait()

    def for_other(n):
        gsend[n] = gate_up(og * units, n).astype(BF16)
        gcopy(n).start()

    loop(nu, for_other)
    for cp in gu_copies[1]:
        cp.wait()
    scopy.wait()
    sums = jnp.sum(ssq[0] + ssq[1], axis=1, keepdims=True)
    ssq[0] = jnp.broadcast_to(lax.rsqrt(sums / width_all + 1e-05), (rows, 128))

    def for_me(n):
        v = gate_up(g * units, n)
        gcopy(n).wait_recv()
        v = v + grecv[n].astype(F32)
        gate = v[:, :128] * ssq[0]
        up = v[:, 128:] * ssq[0]
        hid[g, n] = (gate / (1.0 + jnp.exp(-gate)) * up).astype(BF16)
        hcopy(n).start()

    loop(nu, for_me)
    wd_copy.wait()

    def settle(n):
        remote(hid.at[og, n], hid.at[og, n], hs.at[n], hr.at[n], grp=og).wait_recv()
        gcopy(n).wait_send()
        hcopy(n).wait_send()

    loop(nu, settle)
    for h in range(2):
        for n in range(nu):
            lo = h * units + n * 128
            hcat[:, lo:lo + 128] = hid[h, n]

    def finish_y(n, v):
        v = v + xf[n]
        xf[n] = v

    drain2 = reduce_rows(hcat, wd, psend2, prec2, csend2, crecv2, p2s, p2r, c2s, c2r, finish_y)
    for n in range(nn):
        for h in range(2):
            fin[h, :, n * 512:(n + 1) * 512] = xf[n, 4 * h:4 * h + 4, :].astype(BF16)
    fcopy = remote(fin.at[ok], out_ref.at[k], fs.at[0], fs.at[1], dev=pair)
    fcopy.start()
    out_ref[k] = fin[k]

    def done_attn(i):
        to = lax.rem(d + i + 1, nd)
        remote(abuf.at[:, to], arecv.at[d], as_.at[to], ar.at[d], dev=to).wait_send()

    loop(nd - 1, done_attn)

    def done_gather(i):
        to = lax.rem(c + i + 1, nc)
        remote(xall.at[k, c], xall.at[k, c], ags.at[to], agr.at[c], dev=to * 2 + k).wait_send()

    loop(nc - 1, done_gather)

    def done_forward(i):
        forward(i).wait_send()

    loop(nc, done_forward)
    drain2()
    fcopy.wait()


def fused_device(
    nd, query, key_cache, value_cache, lengths, out_weight, resid, norm_gain,
    gate_weight, up_weight, down_weight,
):
    nc = nd // 2
    rows = nd * 4
    heads = query.shape[1]
    ctx, kvh, hd = key_cache.shape[1:]
    slots = ctx * kvh
    wide = out_weight.shape[1]
    half = wide // 2
    nn = half // 512
    ff = gate_weight.shape[1]
    nu = ff // 256
    keys = key_cache.reshape(2, slots, hd)
    values = value_cache.reshape(2, slots, hd)
    gain = norm_gain.astype(F32).reshape(1, wide)
    vm = pl.BlockSpec(memory_space=pltpu.VMEM)
    hbm = pl.BlockSpec(memory_space=pl.ANY)
    sm = pl.BlockSpec(memory_space=pltpu.SMEM)
    V = pltpu.VMEM
    dma = lambda n: pltpu.SemaphoreType.DMA((n,))
    out = pl.pallas_call(
        functools.partial(layer_kernel, nd),
        out_shape=jax.ShapeDtypeStruct((2, 4, half), BF16),
        in_specs=[sm, vm, hbm, hbm, hbm, vm, vm, hbm, hbm, hbm],
        out_specs=vm,
        scratch_shapes=[
            V((2, slots, hd), BF16), V((2, slots, hd), BF16),
            V(out_weight.shape, BF16), V(gate_weight.shape, BF16),
            V(up_weight.shape, BF16), V(down_weight.shape, BF16),
            V((heads, slots), F32), V((nd, 8, 128), F32), V((2, nd, 8, 128), BF16),
            V((nd, 2, 8, 128), BF16), V((2 * nd * 8, 128), F32),
            V((rows, 512), BF16), V((2, 4, wide), BF16),
            V((nn, nc, 8, 512), BF16), V((nn, nc, 8, 512), BF16), V((nn, nc, 8, 512), F32),
            V((nc, nn, 8, 512), BF16), V((nc, nn, 8, 512), BF16), V((nn, 8, 512), F32),
            V((2, nc, nn, 8, 512), BF16), V((rows, wide), BF16), V((2, rows, 128), F32),
            V((nu, rows, 256), BF16), V((nu, rows, 256), BF16),
            V((2, nu, rows, 128), BF16), V((rows, ff), BF16),
            V((nn, nc, 8, 512), BF16), V((nn, nc, 8, 512), BF16),
            V((nc, nn, 8, 512), BF16), V((nc, nn, 8, 512), BF16), V((2, 4, half), BF16),
            dma(4), dma(6), dma(4), dma(2), dma(nd), dma(nd), dma(nn), dma(nn), dma(nc), dma(nc),
            dma(nc), dma(nc), dma(nc), dma(nc), dma(nu), dma(nu), dma(nu), dma(nu),
            dma(nn), dma(nn), dma(nc), dma(nc), dma(2),
        ],
        compiler_params=pltpu.CompilerParams(
            collective_id=0, has_side_effects=True, vmem_limit_bytes=63 * 1024 * 1024
        ),
        name="decode_layer",
    )(lengths, query, keys, values, out_weight, resid, gain, gate_weight, up_weight, down_weight)
    return jnp.concatenate([out[0], out[1]], axis=1)


def fits(mesh):
    return mesh.shape["grp"] == 2 and mesh.shape["dev"] == 16


def chosen(nd, use, *args):
    query, out_weight, gate_weight = args[0], args[4], args[7]
    same = (
        use and query.shape == (2, 64, 128) and out_weight.shape == (512, 4096)
        and gate_weight.shape[1] % 256 == 0
    )
    return fused_device(nd, *args) if same else per_device(*args)


def solution(mesh):
    placed = (
        P(("grp", "dev"), None, None),
        P(("grp", "dev"), None, None, None),
        P(("grp", "dev"), None, None, None),
        P(("grp", "dev")),
        P("dev", "grp"),
        P("dev", "grp"),
        P("grp"),
        P("grp", "dev"),
        P("grp", "dev"),
        P("dev", "grp"),
    )
    return jax.shard_map(
        functools.partial(chosen, mesh.shape["dev"], fits(mesh)), mesh=mesh, in_specs=placed, out_specs=P("dev", "grp"), check_vma=False
    )
```

```python
import functools

import jax
import jax.numpy as jnp
from jax import lax
from jax.experimental import pallas as pl
from jax.experimental.pallas import tpu as pltpu
from jax.sharding import PartitionSpec as P

MESH = pl.DeviceIdType.MESH
F32 = jnp.float32
BF16 = jnp.bfloat16


def attend(query, key_cache, value_cache, lengths):
    rows, heads, width = query.shape
    kv_heads = key_cache.shape[2]
    group = heads // kv_heads
    grouped = query.reshape(rows, kv_heads, group, width)
    scores = jnp.einsum(
        "rhgd,rlhd->rhgl", grouped, key_cache, preferred_element_type=jnp.float32
    ) * width ** (-0.5)
    places = jnp.arange(key_cache.shape[1], dtype=jnp.int32)
    valid = places[None, :] < lengths[:, None]
    scores = jnp.where(valid[:, None, None, :], scores, -1e30)
    top = jnp.max(scores, axis=-1, keepdims=True)
    weights = jnp.exp(scores - top)
    probs = (weights / jnp.sum(weights, axis=-1, keepdims=True)).astype(jnp.bfloat16)
    mixed = jnp.einsum("rhgl,rlhd->rhgd", probs, value_cache, preferred_element_type=jnp.float32)
    return mixed.reshape(rows, heads * width).astype(jnp.bfloat16)


def per_device(
    query,
    key_cache,
    value_cache,
    lengths,
    out_weight,
    resid,
    norm_gain,
    gate_weight,
    up_weight,
    down_weight,
):
    attn = attend(query, key_cache, value_cache, lengths)
    block_cols = out_weight.shape[0]
    first_col = lax.axis_index("dev") * block_cols
    cols = lax.dynamic_slice_in_dim(
        lax.all_gather(attn, ("grp", "dev"), axis=0, tiled=True), first_col, block_cols, 1
    )
    proj_terms = jnp.dot(cols, out_weight, preferred_element_type=jnp.float32)
    x = resid.astype(jnp.float32) + lax.psum_scatter(
        proj_terms, "dev", scatter_dimension=0, tiled=True
    )
    width_all = x.shape[1] * lax.axis_size("grp")
    sumsq = lax.psum(jnp.sum(x * x, axis=1), "grp")
    normed = (
        x * lax.rsqrt(sumsq / width_all + 1e-05)[:, None] * norm_gain.astype(jnp.float32)
    ).astype(jnp.bfloat16)
    piece = lax.all_gather(normed, "dev", axis=0, tiled=True)
    half_terms = jnp.concatenate(
        [
            jnp.dot(piece, gate_weight, preferred_element_type=jnp.float32),
            jnp.dot(piece, up_weight, preferred_element_type=jnp.float32),
        ],
        axis=1,
    )
    both = lax.psum(half_terms.astype(jnp.bfloat16), "grp").astype(jnp.float32)
    hidden_cols = gate_weight.shape[1]
    gate = both[:, :hidden_cols]
    up = both[:, hidden_cols:]
    hidden = (jax.nn.silu(gate) * up).astype(jnp.bfloat16)
    ffn_rows = lax.psum_scatter(
        jnp.dot(hidden, down_weight, preferred_element_type=jnp.float32),
        "dev",
        scatter_dimension=0,
        tiled=True,
    )
    return (x + ffn_rows).astype(jnp.bfloat16)


def remote(src, dst, send, recv, **where):
    return pltpu.make_async_remote_copy(
        src_ref=src, dst_ref=dst, send_sem=send, recv_sem=recv,
        device_id=where, device_id_type=MESH,
    )


def loop(n, f):
    def step(i, carry):
        f(i)
        return carry

    lax.fori_loop(0, n, step, 0)


def layer_kernel(
    nd,
    len_ref, q_ref, k_hbm, v_hbm, wo_hbm, resid_ref, gain_ref, wg_hbm, wu_hbm, wd_hbm,
    out_ref,
    kb, vb, wo, wg, wu, wd,
    sc, ast, abuf, arecv, af, lhs, rbuf,
    psend, prec, pown, csend, crecv, xf, xall, xg, ssq,
    gsend, grecv, hid, hcat,
    psend2, prec2, csend2, crecv2, fin,
    kvsem, wsem, xs, rs, as_, ar, p1s, p1r, c1s, c1r, ags, agr, fws, fwr, ys, yr,
    gs, gr, hs, hr, p2s, p2r, c2s, c2r, fs,
):
    nc = nd // 2
    g = lax.axis_index("grp")
    d = lax.axis_index("dev")
    c = d // 2
    k = lax.rem(d, 2)
    og = 1 - g
    ok = 1 - k
    pair = c * 2 + ok
    rows = nd * 4
    half = wo.shape[1] // 2
    nn = half // 512
    units = wg.shape[1] // 2
    nu = units // 128
    heads = q_ref.shape[1]
    slots = k_hbm.shape[1]
    width_all = wo.shape[1] * 2

    barrier = pltpu.get_barrier_semaphore()
    all_ = 2 * nd
    me = g * nd + d

    def peer(i):
        t = lax.rem(me + i + 1, all_)
        return t, t // nd, lax.rem(t, nd)

    def greet(i):
        t, tg, td = peer(i)
        pl.semaphore_signal(
            barrier, inc=1, device_id={"grp": tg, "dev": td}, device_id_type=MESH
        )

    loop(all_ - 1, greet)

    kv = []
    for r in range(2):
        kv.append((
            pltpu.make_async_copy(k_hbm.at[r], kb.at[r], kvsem.at[2 * r]),
            pltpu.make_async_copy(v_hbm.at[r], vb.at[r], kvsem.at[2 * r + 1]),
        ))
    for a, b in kv:
        a.start()
        b.start()
    wo_copy = pltpu.make_async_copy(wo_hbm, wo, wsem.at[0])
    wo_copy.start()
    ucols = [pl.ds(pl.multiple_of(og * units, 128), units), pl.ds(pl.multiple_of(g * units, 128), units)]
    gu_copies = []
    for i in range(2):
        gu_copies.append((
            pltpu.make_async_copy(wg_hbm.at[:, ucols[i]], wg.at[:, ucols[i]], wsem.at[1 + 2 * i]),
            pltpu.make_async_copy(wu_hbm.at[:, ucols[i]], wu.at[:, ucols[i]], wsem.at[2 + 2 * i]),
        ))
    wd_copy = pltpu.make_async_copy(wd_hbm, wd, wsem.at[5])

    piece = 1024
    np_ = slots // piece
    for r in range(2):
        kv[r][0].wait()
        q = q_ref[r]
        length = len_ref[r]
        row_head = lax.broadcasted_iota(jnp.int32, (heads, piece), 0) >> 3
        col = lax.broadcasted_iota(jnp.int32, (heads, piece), 1)
        own = (col & 7) == row_head
        place = jnp.where(own, col >> 3, slots)
        top = jnp.full((heads, 1), -1e30, F32)
        for n in range(np_):
            s = lax.dot_general(
                q, kb[r, n * piece:(n + 1) * piece, :], (((1,), (1,)), ((), ())),
                preferred_element_type=F32,
            ) * (128 ** -0.5)
            live = place < length - n * (piece // 8)
            s = jnp.where(live, s, -1e30)
            sc[:, n * piece:(n + 1) * piece] = s
            top = jnp.maximum(top, jnp.max(s, axis=1, keepdims=True))
        kv[r][1].wait()
        if r == 1:
            for a, b in gu_copies:
                a.start()
                b.start()
            wd_copy.start()
        total = jnp.zeros((heads, 1), F32)
        o = jnp.zeros((heads, 128), F32)
        for n in range(np_):
            w = jnp.exp(sc[:, n * piece:(n + 1) * piece] - top)
            total = total + jnp.sum(w, axis=1, keepdims=True)
            o = o + jnp.dot(w.astype(BF16), vb[r, n * piece:(n + 1) * piece, :], preferred_element_type=F32)
        o = o / total
        for t in range(nd):
            ast[t, 4 * r:4 * r + 4, :] = o[4 * t:4 * t + 4, :]
    abuf[...] = ast[...].astype(BF16)

    pl.semaphore_wait(barrier, all_ - 1)

    def send_attn(i):
        t, tg, td = peer(i)
        remote(abuf.at[td], arecv.at[me], as_.at[t], ar.at[me], grp=tg, dev=td).start()

    loop(all_ - 1, send_attn)
    rcopy = remote(resid_ref, rbuf.at[k], rs.at[0], rs.at[1], dev=pair)
    rcopy.start()
    rbuf[k] = resid_ref[...]
    arecv[me] = abuf[d]

    def take_attn(i):
        t, tg, td = peer(i)
        remote(abuf.at[td], arecv.at[t], as_.at[t], ar.at[t], grp=tg, dev=td).wait_recv()

    loop(all_ - 1, take_attn)
    wo_copy.wait()
    af[...] = arecv[...].astype(F32).reshape(all_ * 8, 128)
    for j in range(4):
        lhs[:, j * 128:(j + 1) * 128] = af[pl.ds(j, rows, stride=4), :].astype(BF16)

    def reduce_rows(left, w, ps, pr, cs, cr, pss, prs, css, crs, finish):
        def other(n):
            cols = pl.ds(pl.multiple_of(ok * half + n * 512, 512), 512)
            v = jnp.dot(left[...], w[:, cols], preferred_element_type=F32)
            ps[n] = v.reshape(nc, 8, 512).astype(BF16)
            remote(ps.at[n], pr.at[n], pss.at[n], prs.at[n], dev=pair).start()

        def part(n, to):
            return remote(
                cs.at[n, to], cr.at[n, c], css.at[n * nc + to], crs.at[n * nc + c], dev=to * 2 + k
            )

        def arrived(n, frm):
            return remote(
                cs.at[n, frm], cr.at[n, frm], css.at[n * nc + frm], crs.at[n * nc + frm],
                dev=frm * 2 + k,
            )

        def mine(n):
            cols = pl.ds(pl.multiple_of(k * half + n * 512, 512), 512)
            v = jnp.dot(left[...], w[:, cols], preferred_element_type=F32)
            remote(ps.at[n], pr.at[n], pss.at[n], prs.at[n], dev=pair).wait_recv()
            v = v.reshape(nc, 8, 512) + pr[n].astype(F32)
            pown[n] = v
            cs[n] = v.astype(BF16)
            loop(nc - 1, lambda i: part(n, lax.rem(c + i + 1, nc)).start())

        def both(n):
            other(n + 1)
            mine(n)

        other(0)
        loop(nn - 1, both)
        mine(nn - 1)

        def total(n):
            loop(nc - 1, lambda i: arrived(n, lax.rem(c + i + 1, nc)).wait_recv())
            v = pown[n, c]
            for i in range(1, nc):
                v = v + cr[n, lax.rem(c + i, nc)].astype(F32)
            finish(n, v)

        loop(nn, total)

        def done_pair(n):
            remote(ps.at[n], pr.at[n], pss.at[n], prs.at[n], dev=pair).wait_send()

        def done(j):
            part(j // (nc - 1), lax.rem(c + 1 + lax.rem(j, nc - 1), nc)).wait_send()

        def drain():
            loop(nn, done_pair)
            loop(nn * (nc - 1), done)

        return drain

    rcopy.wait()

    nz = nc // 2
    yc = c + 1 - 2 * lax.rem(c, 2)

    def along_z(n, to):
        return remote(xall.at[k, n, c], xall.at[k, n, c], ags.at[n * nc + to], agr.at[n * nc + c], dev=to * 2 + k)

    def from_z(n, frm):
        return remote(xall.at[k, n, frm], xall.at[k, n, frm], ags.at[n * nc + frm], agr.at[n * nc + frm], dev=frm * 2 + k)

    def along_y(n, frm):
        return remote(xall.at[k, n, frm], xall.at[k, n, frm], ys.at[n * nc + frm], yr.at[n * nc + frm], dev=yc * 2 + k)

    def forward(n, frm):
        return remote(xall.at[k, n, frm], xall.at[k, n, frm], fws.at[n * nc + frm], fwr.at[n * nc + frm], dev=pair)

    def finish_x(n, v):
        cols = pl.ds(pl.multiple_of(k * half + n * 512, 512), 512)
        for h in range(2):
            xf[n, 4 * h:4 * h + 4, :] = rbuf[h, :, cols].astype(F32)
        v = v + xf[n]
        xf[n] = v
        xall[k, n, c] = (v * gain_ref[:, cols].astype(F32)).astype(BF16)
        loop(nz - 1, lambda i: along_z(n, lax.rem(c + 2 * i + 2, nc)).start())
        along_y(n, c).start()
        forward(n, c).start()

    drain1 = reduce_rows(lhs, wo, psend, prec, csend, crecv, p1s, p1r, c1s, c1r, finish_x)

    def z_take(n):
        def one(i):
            frm = lax.rem(c + 2 * i + 2, nc)
            from_z(n, frm).wait_recv()
            along_y(n, frm).start()
            forward(n, frm).start()

        loop(nz - 1, one)

    def y_take(n):
        def one(i):
            frm = lax.rem(yc + 2 * i, nc)
            along_y(n, frm).wait_recv()
            forward(n, frm).start()

        loop(nz, one)

    def build(h, n):
        cols = pl.ds(pl.multiple_of(h * half + n * 512, 512), 512)
        v = xall[h, n].astype(F32).reshape(rows, 512)
        xg[:, cols] = v.astype(BF16)
        v = v * (1.0 / gain_ref[:, cols].astype(F32))
        v = v * v
        ssq[g] += (v[:, :128] + v[:, 128:256]) + (v[:, 256:384] + v[:, 384:])

    ssq[g] = jnp.zeros((rows, 128), F32)
    z_take(0)

    def stage(n):
        z_take(n + 1)
        y_take(n)
        build(k, n)

    loop(nn - 1, stage)
    y_take(nn - 1)
    build(k, nn - 1)

    def pair_half(n):
        def one(i):
            remote(xall.at[ok, n, i], xall.at[ok, n, i], fws.at[n * nc + i], fwr.at[n * nc + i], dev=pair).wait_recv()

        loop(nc, one)
        build(ok, n)

    loop(nn, pair_half)
    drain1()
    scopy = remote(ssq.at[g], ssq.at[g], xs.at[2], xs.at[3], grp=og)
    scopy.start()

    def gate_up(base, n):
        cols = pl.ds(pl.multiple_of(base + n * 128, 128), 128)
        both = jnp.concatenate([wg[:, cols], wu[:, cols]], axis=1)
        return jnp.dot(xg[...], both, preferred_element_type=F32)

    def gcopy(n):
        return remote(gsend.at[n], grecv.at[n], gs.at[n], gr.at[n], grp=og)

    def hcopy(n):
        return remote(hid.at[g, n], hid.at[g, n], hs.at[n], hr.at[n], grp=og)

    for cp in gu_copies[0]:
        cp.wait()

    def for_other(n):
        gsend[n] = gate_up(og * units, n).astype(BF16)
        gcopy(n).start()

    loop(nu, for_other)
    for cp in gu_copies[1]:
        cp.wait()
    scopy.wait()
    sums = jnp.sum(ssq[0] + ssq[1], axis=1, keepdims=True)
    ssq[0] = jnp.broadcast_to(lax.rsqrt(sums / width_all + 1e-05), (rows, 128))

    def for_me(n):
        v = gate_up(g * units, n)
        gcopy(n).wait_recv()
        v = v + grecv[n].astype(F32)
        gate = v[:, :128] * ssq[0]
        up = v[:, 128:] * ssq[0]
        hid[g, n] = (gate / (1.0 + jnp.exp(-gate)) * up).astype(BF16)
        hcopy(n).start()

    loop(nu, for_me)
    wd_copy.wait()

    def settle(n):
        remote(hid.at[og, n], hid.at[og, n], hs.at[n], hr.at[n], grp=og).wait_recv()
        gcopy(n).wait_send()
        hcopy(n).wait_send()

    loop(nu, settle)
    for h in range(2):
        for n in range(nu):
            lo = h * units + n * 128
            hcat[:, lo:lo + 128] = hid[h, n]

    def finish_y(n, v):
        v = v + xf[n]
        xf[n] = v

    drain2 = reduce_rows(hcat, wd, psend2, prec2, csend2, crecv2, p2s, p2r, c2s, c2r, finish_y)
    for n in range(nn):
        for h in range(2):
            fin[h, :, n * 512:(n + 1) * 512] = xf[n, 4 * h:4 * h + 4, :].astype(BF16)
    mycols = pl.ds(pl.multiple_of(k * half, 512), half)
    fcopy = remote(fin.at[ok], out_ref.at[:, mycols], fs.at[0], fs.at[1], dev=pair)
    fcopy.start()
    out_ref[:, mycols] = fin[k]

    def done_attn(i):
        t, tg, td = peer(i)
        remote(abuf.at[td], arecv.at[me], as_.at[t], ar.at[me], grp=tg, dev=td).wait_send()

    loop(all_ - 1, done_attn)

    def done_gather(n):
        loop(nz - 1, lambda i: along_z(n, lax.rem(c + 2 * i + 2, nc)).wait_send())
        loop(nz, lambda i: along_y(n, lax.rem(c + 2 * i, nc)).wait_send())
        loop(nc, lambda i: forward(n, i).wait_send())

    loop(nn, done_gather)
    drain2()
    fcopy.wait()


def fused_device(
    nd, query, key_cache, value_cache, lengths, out_weight, resid, norm_gain,
    gate_weight, up_weight, down_weight,
):
    nc = nd // 2
    rows = nd * 4
    heads = query.shape[1]
    ctx, kvh, hd = key_cache.shape[1:]
    slots = ctx * kvh
    wide = out_weight.shape[1]
    half = wide // 2
    nn = half // 512
    ff = gate_weight.shape[1]
    nu = ff // 256
    keys = key_cache.reshape(2, slots, hd)
    values = value_cache.reshape(2, slots, hd)
    gain = norm_gain.reshape(1, wide)
    vm = pl.BlockSpec(memory_space=pltpu.VMEM)
    hbm = pl.BlockSpec(memory_space=pl.ANY)
    sm = pl.BlockSpec(memory_space=pltpu.SMEM)
    V = pltpu.VMEM
    dma = lambda n: pltpu.SemaphoreType.DMA((n,))
    out = pl.pallas_call(
        functools.partial(layer_kernel, nd),
        out_shape=jax.ShapeDtypeStruct((4, wide), BF16),
        in_specs=[sm, vm, hbm, hbm, hbm, vm, vm, hbm, hbm, hbm],
        out_specs=vm,
        scratch_shapes=[
            V((2, slots, hd), BF16), V((2, slots, hd), BF16),
            V(out_weight.shape, BF16), V(gate_weight.shape, BF16),
            V(up_weight.shape, BF16), V(down_weight.shape, BF16),
            V((heads, slots), F32), V((nd, 8, 128), F32), V((nd, 8, 128), BF16),
            V((2 * nd, 8, 128), BF16), V((2 * nd * 8, 128), F32),
            V((rows, 512), BF16), V((2, 4, wide), BF16),
            V((nn, nc, 8, 512), BF16), V((nn, nc, 8, 512), BF16), V((nn, nc, 8, 512), F32),
            V((nn, nc, 8, 512), BF16), V((nn, nc, 8, 512), BF16), V((nn, 8, 512), F32),
            V((2, nn, nc, 8, 512), BF16), V((rows, wide), BF16), V((2, rows, 128), F32),
            V((nu, rows, 256), BF16), V((nu, rows, 256), BF16),
            V((2, nu, rows, 128), BF16), V((rows, ff), BF16),
            V((nn, nc, 8, 512), BF16), V((nn, nc, 8, 512), BF16),
            V((nn, nc, 8, 512), BF16), V((nn, nc, 8, 512), BF16), V((2, 4, half), BF16),
            dma(4), dma(6), dma(4), dma(2), dma(2 * nd), dma(2 * nd), dma(nn), dma(nn),
            *[dma(nn * nc) for _ in range(8)], dma(nu), dma(nu), dma(nu), dma(nu),
            dma(nn), dma(nn), dma(nn * nc), dma(nn * nc), dma(2),
        ],
        compiler_params=pltpu.CompilerParams(
            collective_id=0, has_side_effects=True, vmem_limit_bytes=63 * 1024 * 1024
        ),
        name="decode_layer",
    )(lengths, query, keys, values, out_weight, resid, gain, gate_weight, up_weight, down_weight)
    return out


def fits(mesh):
    return mesh.shape["grp"] == 2 and mesh.shape["dev"] == 16


def chosen(nd, use, *args):
    query, out_weight, gate_weight = args[0], args[4], args[7]
    same = (
        use and query.shape == (2, 64, 128) and out_weight.shape == (512, 4096)
        and gate_weight.shape[1] % 256 == 0
    )
    return fused_device(nd, *args) if same else per_device(*args)


def solution(mesh):
    placed = (
        P(("grp", "dev"), None, None),
        P(("grp", "dev"), None, None, None),
        P(("grp", "dev"), None, None, None),
        P(("grp", "dev")),
        P("dev", "grp"),
        P("dev", "grp"),
        P("grp"),
        P("grp", "dev"),
        P("grp", "dev"),
        P("dev", "grp"),
    )
    return jax.shard_map(
        functools.partial(chosen, mesh.shape["dev"], fits(mesh)), mesh=mesh, in_specs=placed, out_specs=P("dev", "grp"), check_vma=False
    )
```
